32 devices in a mesh: blk: 16 (over z, y, core), tok: 2 (over x).
Axes of the slice: x: 2, y: 2, z: 4, core: 2. Of those that a mesh axis runs over, the one named last changes fastest.
Arguments:
- tokens: bfloat16 [64, 8192], P(('blk', 'tok')), may hold values from -6 to 6
- upstream: bfloat16 [64, 8192], P(('blk', 'tok')), may hold values from -6 to 6
- gate_weight: bfloat16 [14336, 8192], P('blk'), may hold values from -0.0625 to 0.0625
- up_weight: bfloat16 [14336, 8192], P('blk'), may hold values from -0.0625 to 0.0625
- down_weight: bfloat16 [14336, 8192], P('blk'), may hold values from -0.046875 to 0.046875
Outputs:
- mixed: bfloat16 [64, 8192], P(('blk', 'tok'))
- input_grad: bfloat16 [64, 8192], P(('blk', 'tok'))
- gate_weight_grad: bfloat16 [14336, 8192], P('blk', 'tok')
- up_weight_grad: bfloat16 [14336, 8192], P('blk', 'tok')
- down_weight_grad: bfloat16 [14336, 8192], P('blk', 'tok')
The draws below stay inside these ranges and needn't reach their ends.
All inputs are finite; a program needn't handle non-finite values.
Results may differ from the reference program's by a relative error of at most 0.0049.
Values may be sent and summed in bfloat16 or wider, within the bound.
A program may use at most 192 MiB of HBM per device.

```python
import jax
import jax.numpy as jnp

D = 8192
FF = 14336
TOKENS = 64


def level_of(own_key, extent, shards, low, high):
    gain = 1.0
    for dim, shards_of in shards:
        draws = jax.random.uniform(jax.random.fold_in(jax.random.fold_in(own_key, 6), dim), (shards_of,), jnp.float32, low / len(shards), high / len(shards))
        gain = gain * jnp.repeat(jnp.exp(draws), extent[dim] // shards_of).reshape((-1,) + (1,) * (len(extent) - 1 - dim))
    return gain


def noise(own_key, shape, scale, most, pieces=(), kind=jnp.bfloat16):
    level = level_of(own_key, shape, pieces, -0.22, 0.18) if pieces else 1.0
    drawn = jax.random.normal(own_key, shape, jnp.float32) * scale * level
    return jnp.minimum(jnp.maximum(drawn, -most), most).astype(kind)


def setup_inputs(seed: int = 0) -> dict:
    streams_of = jax.random.split(jax.random.key(seed), 6)
    tokens = noise(streams_of[0], (TOKENS, D), 1.0, 6.0, ((0, 32),))
    upstream = noise(streams_of[1], (TOKENS, D), 1.0, 6.0, ((0, 32),))
    gate_weight = noise(streams_of[2], (FF, D), D ** -0.5, 0.0625, ((0, 16),))
    up_weight = noise(streams_of[3], (FF, D), D ** -0.5, 0.0625, ((0, 16),))
    down_weight = noise(streams_of[4], (FF, D), FF ** -0.5, 0.046875, ((0, 16),))
    return dict(tokens=tokens, upstream=upstream, gate_weight=gate_weight, up_weight=up_weight, down_weight=down_weight)


def reference(tokens, upstream, gate_weight, up_weight, down_weight):
    gate_value = jnp.dot(tokens, gate_weight.T, preferred_element_type=jnp.float32)
    up_value = jnp.dot(tokens, up_weight.T, preferred_element_type=jnp.float32)
    gate_sigmoid = jax.nn.sigmoid(gate_value)
    swish_gate = gate_value * gate_sigmoid
    hidden = (swish_gate * up_value).astype(jnp.bfloat16)
    mixed = jnp.dot(hidden, down_weight, preferred_element_type=jnp.float32).astype(jnp.bfloat16)
    hidden_grad = jnp.dot(upstream, down_weight.T, preferred_element_type=jnp.float32)
    gate_grad = (hidden_grad * up_value * gate_sigmoid * (1.0 + gate_value * (1.0 - gate_sigmoid))).astype(jnp.bfloat16)
    up_grad = (hidden_grad * swish_gate).astype(jnp.bfloat16)
    input_sum = jnp.dot(gate_grad, gate_weight, preferred_element_type=jnp.float32)
    input_sum = input_sum + jnp.dot(up_grad, up_weight, preferred_element_type=jnp.float32)
    input_grad = input_sum.astype(jnp.bfloat16)
    gate_weight_grad = jnp.dot(gate_grad.T, tokens, preferred_element_type=jnp.float32).astype(jnp.bfloat16)
    up_weight_grad = jnp.dot(up_grad.T, tokens, preferred_element_type=jnp.float32).astype(jnp.bfloat16)
    down_weight_grad = jnp.dot(hidden.T, upstream, preferred_element_type=jnp.float32).astype(jnp.bfloat16)
    return mixed, input_grad, gate_weight_grad, up_weight_grad, down_weight_grad
```

```python
import jax
import jax.numpy as jnp
from jax import lax
from jax.sharding import PartitionSpec as P


def swapped(block, axis, distance):
    count = lax.axis_size(axis)
    route = []
    for low in range(count):
        high = low | 1 << distance
        if high != low and high < count:
            route += [(low, high), (high, low)]
    return lax.ppermute(block, axis, route)


def right_product(left, right):
    return lax.dot_general(
        left, right, (((1,), (1,)), ((), ())), preferred_element_type=jnp.float32
    )


def left_product(left, right):
    return lax.dot_general(
        left, right, (((0,), (0,)), ((), ())), preferred_element_type=jnp.float32
    )


def rounds(axis):
    count = lax.axis_size(axis)
    levels = count.bit_length() - 1
    assert count == 1 << levels
    return range(levels)


def gathered(block, axis):
    for distance in reversed(rounds(axis)):
        block = jnp.concatenate([block, swapped(block, axis, distance)], axis=0)
    return block


def scattered(term, axis):
    for distance in rounds(axis):
        half = term.shape[0] // 2
        term = term[:half] + swapped(
            term[half:].astype(jnp.bfloat16), axis, distance
        ).astype(jnp.float32)
    return term


def local(tokens, upstream, gate_weight, up_weight, down_weight):
    rows_in = gathered(tokens, "blk")
    grads_in = gathered(upstream, "blk")
    width = rows_in.shape[1]
    half_width = width // 2
    tok_index = lax.axis_index("tok")
    own_start = tok_index * half_width
    other_start = (1 - tok_index) * half_width

    def both_groups(rows):
        own = lax.dynamic_slice_in_dim(rows, own_start, half_width, 1)
        sent = lax.dynamic_slice_in_dim(rows, other_start, half_width, 1)
        return jnp.concatenate([own, swapped(sent, "tok", 0)], axis=0)

    gate_value = right_product(rows_in, gate_weight)
    up_value = right_product(rows_in, up_weight)
    gate_sigmoid = jax.nn.sigmoid(gate_value)
    swish_gate = gate_value * gate_sigmoid
    hidden = (swish_gate * up_value).astype(jnp.bfloat16)
    hidden_grad = right_product(grads_in, down_weight)
    gate_grad = (
        hidden_grad * up_value * gate_sigmoid * (1.0 + gate_value * (1.0 - gate_sigmoid))
    ).astype(jnp.bfloat16)
    up_grad = (hidden_grad * swish_gate).astype(jnp.bfloat16)
    output_term = jnp.dot(hidden, down_weight, preferred_element_type=jnp.float32)
    input_term = jnp.dot(gate_grad, gate_weight, preferred_element_type=jnp.float32) + jnp.dot(
        up_grad, up_weight, preferred_element_type=jnp.float32
    )
    mixed = scattered(output_term, "blk").astype(jnp.bfloat16)
    input_grad = scattered(input_term, "blk").astype(jnp.bfloat16)
    all_rows = both_groups(rows_in)
    all_grads = both_groups(grads_in)
    all_hidden, all_gate, all_up = (
        jnp.concatenate([part, swapped(part, "tok", 0)], axis=0)
        for part in (hidden, gate_grad, up_grad)
    )
    return (
        mixed,
        input_grad,
        left_product(all_gate, all_rows).astype(jnp.bfloat16),
        left_product(all_up, all_rows).astype(jnp.bfloat16),
        left_product(all_hidden, all_grads).astype(jnp.bfloat16),
    )


def solution(mesh):
    return jax.shard_map(
        local,
        mesh=mesh,
        in_specs=(
            P(("blk", "tok"), None),
            P(("blk", "tok"), None),
            P("blk", None),
            P("blk", None),
            P("blk", None),
        ),
        out_specs=(
            P(("blk", "tok"), None),
            P(("blk", "tok"), None),
            P("blk", "tok"),
            P("blk", "tok"),
            P("blk", "tok"),
        ),
        check_vma=False,
    )
```
